512 devices in a mesh: rows: 64 (over x, y, core), cols: 8 (over z).
Axes of the slice: x: 4, y: 8, z: 8, core: 2. Of those that a mesh axis runs over, the one named last changes fastest.
Arguments:
- eigvecs: float32 [65536, 2048], P(('rows', 'cols')), may hold values from -6 to 6
- panels: float32 [8, 65536, 256], P('cols', 'rows'), may hold values from -0.375 to 0.375
- tfactors: float32 [2, 256, 256], replicated, may hold values from -0.03125 to 0.03125
- owners: int32 [2], replicated, may hold values from 0 to 7, as said below
Outputs:
- backvecs: float32 [65536, 2048], P('rows', 'cols')
The draws below stay inside these ranges and needn't reach their ends.
Inputs may be any that keep to these rules, and one draw needn't show every extreme that they name: `owners`: the entries are distinct slots, among them 0 and 7.
All inputs are finite; a program needn't handle non-finite values.
Results may differ from the reference program's by a relative error of at most 0.00011.
Values sent between devices are 32-bit elements; how exact they have to be, the bound alone decides.
No kernel may reach another device: no remote copies, remote signals or barrier semaphores. Data moves between devices by JAX's collectives and lax.ppermute only.
A program may use at most 64 MiB of HBM per device.

```python
import jax
import jax.numpy as jnp
from jax import lax

N = 65536
K = 2048
W = 256
PANELS = 2
STORE = 8


def draw_owners(key, part):
    first_key = jax.random.fold_in(key, 11)
    second_key = jax.random.fold_in(key, 12)
    others = (jax.random.permutation(first_key, STORE - 2) + 1).astype(jnp.int32)
    ends = jnp.array([0, STORE - 1], jnp.int32)
    picked = jnp.concatenate([ends, others[:PANELS - 2]])
    order = jax.random.permutation(second_key, PANELS).astype(jnp.int32)
    return picked[order]


def level_of(key, dims, cuts, low, largest):
    factor_of, own = 1.0, jax.random.fold_in(key, 6)
    for axis_at, parts in cuts:
        draws = jnp.exp(jax.random.uniform(jax.random.fold_in(own, axis_at), (parts,), jnp.float32, low / len(cuts), largest / len(cuts)))
        factor_of = factor_of * jnp.repeat(draws, dims[axis_at] // parts).reshape([-1 if axis == axis_at else 1 for axis in range(len(dims))])
    return factor_of


def normal_values(key, shape, deviation, bound, split=(), kind=jnp.bfloat16):
    values = deviation * jax.random.normal(key, shape, jnp.float32)
    if split:
        values = values * level_of(key, shape, split, -0.22, 0.18)
    return jnp.clip(values, -bound, bound).astype(kind)


def setup_inputs(seed: int = 0) -> dict:
    key_of = jax.random.split(jax.random.key(seed), 5)
    eigvecs = normal_values(key_of[0], (N, K), 1.0, 6.0, ((0, 512),), jnp.float32)
    panels = normal_values(key_of[1], (STORE, N, W), W ** -0.5, 0.375, ((0, 8), (1, 64)), jnp.float32)
    tfactors = normal_values(key_of[2], (PANELS, W, W), (N // 2) ** -0.5, 0.03125, (), jnp.float32)
    owners = draw_owners(jax.random.fold_in(key_of[4], 71), 0)
    return {"eigvecs": eigvecs, "panels": panels, "tfactors": tfactors, "owners": owners}


def reference(eigvecs, panels, tfactors, owners):
    result = eigvecs
    for index in range(PANELS):
        vector = lax.dynamic_index_in_dim(panels, owners[index], 0, keepdims=False)
        factor = jnp.triu(tfactors[index])
        proj = jnp.dot(vector.T, result, precision=lax.Precision.HIGHEST, preferred_element_type=jnp.float32)
        coeff = jnp.dot(factor, proj, precision=lax.Precision.HIGHEST, preferred_element_type=jnp.float32)
        result = result - jnp.dot(vector, coeff, precision=lax.Precision.HIGHEST, preferred_element_type=jnp.float32)
    return result
```

```python
import jax
import jax.numpy as jnp
from jax import lax
from jax.sharding import Mesh, PartitionSpec as P

HIGHEST = lax.Precision.HIGHEST
PLANE = ("x", "y")


def dot(left, right, dims):
    return lax.dot_general(left, right, (dims, ((), ())), precision=HIGHEST, preferred_element_type=jnp.float32)


def tn(left, right):
    return dot(left, right, ((0,), (0,)))


def nn(left, right):
    return dot(left, right, ((1,), (0,)))


def gather_panels(local, owners):
    rows = local.shape[0]
    quarter = rows // 4
    slot = lax.axis_index("z")
    last = lax.axis_size("z") - 1
    half = (last + 1) // 2
    mine = lax.dynamic_slice_in_dim(local, jnp.where(slot == last, rows - quarter, 0), quarter)
    chunk = mine
    for step in range(1, half):
        start = jnp.where(slot == last, (half - 1 - step) * quarter, step * quarter)
        piece = lax.dynamic_slice_in_dim(local, start, quarter)
        piece = lax.ppermute(piece, "z", [(0, step), (last, last - step)])
        chunk = jnp.where((slot == step) | (slot == last - step), piece, chunk)
    both = lax.all_gather(chunk, "z", axis=0, tiled=True).reshape(2, rows, local.shape[1])
    lead = jnp.where(owners[0] == 0, 0, 1)
    return lax.dynamic_index_in_dim(both, lead, 0, False), lax.dynamic_index_in_dim(both, 1 - lead, 0, False)


def reduce_rows(part):
    rows, columns = part.shape
    pairs = lax.axis_size("c")
    planes = lax.axis_size("x") * lax.axis_size("y")
    part = lax.all_to_all(part, "c", split_axis=0, concat_axis=0, tiled=True)
    part = part.reshape(pairs, rows // pairs, columns).sum(0)
    tiles = part.reshape(rows // pairs // 8, 8, columns // 128, 128).transpose(0, 2, 1, 3)
    tiles = tiles.reshape(planes, -1, 8, 128)
    tiles = lax.all_to_all(tiles, PLANE, split_axis=0, concat_axis=0, tiled=True)
    total = tiles.sum(0)
    tiles = jnp.broadcast_to(total[None], tiles.shape)
    tiles = lax.all_to_all(tiles, PLANE, split_axis=0, concat_axis=0, tiled=True)
    tiles = tiles.reshape(rows // pairs // 8, columns // 128, 8, 128).transpose(0, 2, 1, 3)
    return lax.all_gather(tiles.reshape(rows // pairs, columns), "c", axis=0, tiled=True)


def per_device(eigvecs, panels, tfactors, owners):
    first, second = gather_panels(panels[0], owners)
    tiles = lax.all_to_all(eigvecs, "z", split_axis=1, concat_axis=0, tiled=True)
    width = first.shape[1]
    total = reduce_rows(jnp.concatenate([tn(first, tiles), tn(second, tiles), tn(second, first)]))
    proj_first, proj_second, cross = total[:width], total[width : 2 * width], total[2 * width :]
    coeff_first = nn(jnp.triu(tfactors[0]), proj_first)
    coeff_second = nn(jnp.triu(tfactors[1]), proj_second - nn(cross, coeff_first))
    return tiles - nn(first, coeff_first) - nn(second, coeff_second)


def solution(mesh):
    split = Mesh(mesh.devices.reshape(4, 8, 2, 8), ("x", "y", "c", "z"))
    rows = ("x", "y", "c")
    placed = (P(rows + ("z",), None), P("z", rows, None), P(), P())
    return jax.shard_map(per_device, mesh=split, in_specs=placed, out_specs=P(rows, "z"), check_vma=False)
```

```python
import jax
import jax.numpy as jnp
from jax import lax
from jax.sharding import Mesh, PartitionSpec as P

PLANE = ("x", "y")


def dot(left, right, dims):
    return lax.dot_general(
        left, right, (dims, ((), ())), precision=lax.Precision.HIGH, preferred_element_type=jnp.float32
    )


def tn(left, right):
    return dot(left, right, ((0,), (0,)))


def nn(left, right):
    return dot(left, right, ((1,), (0,)))


def shift(value, by):
    count = lax.axis_size("z")
    return lax.ppermute(value, "z", [(slot, (slot + by) % count) for slot in range(count)])


def owner_quarters(local):
    quarter = local.shape[0] // 4
    last = lax.axis_index("z") == lax.axis_size("z") - 1
    starts = [jnp.where(last, (3 - step) * quarter, step * quarter) for step in range(4)]
    return [lax.dynamic_slice_in_dim(local, start, quarter) for start in starts]


def scatter_quarters(pieces):
    slot = lax.axis_index("z")
    last = lax.axis_size("z") - 1
    chunk = pieces[0]
    for step in range(1, 4):
        piece = lax.ppermute(pieces[step], "z", [(0, step), (last, last - step)])
        chunk = jnp.where((slot == step) | (slot == last - step), piece, chunk)
    return chunk


def gather_panels(chunk):
    rows, width = chunk.shape
    before2, after2 = shift(chunk, 2), shift(chunk, -2)
    before1, after1 = shift(chunk, 1), shift(chunk, -1)
    after3, before3 = shift(after2, -1), shift(before2, 1)
    across = jnp.concatenate([shift(after2[: rows // 2], -2), shift(before2[rows // 2 :], 2)])
    before, after = [chunk, before1, before2, before3], [chunk, after1, after2, after3]
    slot = lax.axis_index("z")
    both = jnp.zeros((8, rows, width), chunk.dtype)
    for by, piece in enumerate(before):
        both = lax.dynamic_update_index_in_dim(both, piece, (slot - by) % 8, 0)
    for by, piece in enumerate(after[1:]):
        both = lax.dynamic_update_index_in_dim(both, piece, (slot + by + 1) % 8, 0)
    both = lax.dynamic_update_index_in_dim(both, across, (slot + 4) % 8, 0)
    return both.reshape(2, 4 * rows, width)


def products(first, second, tiles, half):
    width = tiles.shape[1] // 2
    tiles, other = (lax.dynamic_slice_in_dim(value, half * width, width, 1) for value in (tiles, first))
    return jnp.concatenate([tn(first, tiles), tn(second, tiles), tn(second, other)])


def reduce_rows(first, second, tiles):
    core = lax.axis_index("c")
    other = products(first, second, tiles, 1 - core)
    other = lax.ppermute(other, "c", [(0, 1), (1, 0)])
    part = products(first, second, tiles, core) + other
    rows, columns = part.shape
    planes = lax.axis_size("x") * lax.axis_size("y")
    pieces = part.reshape(planes, rows // planes, columns)
    pieces = lax.all_to_all(pieces, PLANE, split_axis=0, concat_axis=0, tiled=True)
    pieces = jnp.broadcast_to(pieces.sum(0)[None], pieces.shape)
    pieces = lax.all_to_all(pieces, PLANE, split_axis=0, concat_axis=0, tiled=True)
    return lax.all_gather(pieces.reshape(rows, columns), "c", axis=1, tiled=True)


def per_device(eigvecs, panels, tfactors, owners):
    pieces = owner_quarters(panels[0])
    pieces, eigvecs = lax.optimization_barrier((pieces, eigvecs))
    chunk = scatter_quarters(pieces)
    factors = jnp.triu(tfactors)
    count = lax.axis_size("z")
    tiles = eigvecs.reshape(eigvecs.shape[0], count, -1).swapaxes(0, 1)
    chunk, tiles, factors = lax.optimization_barrier((chunk, tiles, factors))
    tiles = lax.all_to_all(tiles, "z", split_axis=0, concat_axis=0, tiled=True)
    tiles = tiles.reshape(-1, tiles.shape[2])
    both = gather_panels(chunk)
    lead = jnp.where(owners[0] == 0, 0, 1)
    first = lax.dynamic_index_in_dim(both, lead, 0, False)
    second = lax.dynamic_index_in_dim(both, 1 - lead, 0, False)
    width = first.shape[1]
    total = reduce_rows(first, second, tiles)
    proj_first, proj_second, cross = total[:width], total[width : 2 * width], total[2 * width :]
    coeff_first = nn(factors[0], proj_first)
    coeff_second = nn(factors[1], proj_second - nn(cross, coeff_first))
    return tiles - nn(first, coeff_first) - nn(second, coeff_second)


def solution(mesh):
    split = Mesh(mesh.devices.reshape(4, 8, 2, 8), ("x", "y", "c", "z"))
    rows = ("x", "y", "c")
    placed = (P(rows + ("z",), None), P("z", rows, None), P(), P())
    return jax.shard_map(per_device, mesh=split, in_specs=placed, out_specs=P(rows, "z"), check_vma=False)
```

```python
import jax
import jax.numpy as jnp
from jax import lax
from jax.experimental import pallas as pl
from jax.experimental.pallas import tpu as pltpu
from jax.sharding import Mesh, PartitionSpec as P

PLANE = ("x", "y")
TN = (((0,), (0,)), ((), ()))
NN = (((1,), (0,)), ((), ()))
VMEM = pl.BlockSpec(memory_space=pltpu.VMEM)
LIMIT = 16 * 1024 * 1024
SMEM = pl.BlockSpec(memory_space=pltpu.SMEM)


def parts(value):
    high = value.astype(jnp.bfloat16)
    return high, (value - high.astype(jnp.float32)).astype(jnp.bfloat16)


def product(left, right, dims):
    def one(a, b):
        return lax.dot_general(a, b, dims, preferred_element_type=jnp.float32)

    return one(left[0], right[0]) + (one(left[0], right[1]) + one(left[1], right[0]))


def quarters(where_ref, chunks):
    slot, lead = where_ref[0], where_ref[1]
    for k in range(4):
        near = chunks[k][...]
        far = chunks[k + 4][...] if k else jnp.concatenate([chunks[4][...], chunks[8][...]])
        place = lax.rem(slot + k, 8)
        row = pl.multiple_of(lax.rem(place, 4) * 256, 256)
        yield row, jnp.where(place < 4, 0, 1) == lead, near, far


def cross_kernel(where_ref, *refs):
    chunks, cross_ref = refs[:9], refs[9]
    for k, (row, leads, near, far) in enumerate(quarters(where_ref, chunks)):
        term = product(parts(jnp.where(leads, far, near)), parts(jnp.where(leads, near, far)), TN)
        if k == 0:
            cross_ref[...] = term
        else:
            cross_ref[...] += term


def products_kernel(where_ref, cross_ref, *refs):
    chunks, (tiles_ref, other_ref, mine_ref, total_ref) = refs[:9], refs[9:]
    for k, (row, leads, near, far) in enumerate(quarters(where_ref, chunks)):
        tile = parts(tiles_ref[pl.ds(row, 256), :])
        for at, panel in enumerate((jnp.where(leads, near, far), jnp.where(leads, far, near))):
            term = product(parts(panel), tile, TN)
            if k == 0:
                total_ref[at] = term
            else:
                total_ref[at] += term
    mine = where_ref[2]
    for ref, half in ((other_ref, 1 - mine), (mine_ref, mine)):
        lanes = pl.ds(pl.multiple_of(half * 128, 128), 128)
        for at in range(2):
            ref[pl.ds(at * 256, 256), :] = total_ref[at, :, lanes]
        ref[pl.ds(512, 256), :] = cross_ref[:, lanes]


def update_kernel(where_ref, *refs):
    chunks, (tiles_ref, total_ref, factors_ref, out_ref) = refs[:9], refs[9:]
    upper = lax.broadcasted_iota(jnp.int32, (256, 256), 0) <= lax.broadcasted_iota(jnp.int32, (256, 256), 1)
    first, second = (parts(jnp.where(upper, factors_ref[at], 0.0)) for at in range(2))
    lead_coeff = product(first, parts(total_ref[0:256]), NN)
    lead_parts = parts(lead_coeff)
    trail = total_ref[256:512] - product(parts(total_ref[512:768]), lead_parts, NN)
    trail_parts = parts(product(second, parts(trail), NN))
    for row, leads, near, far in quarters(where_ref, chunks):
        lead = parts(jnp.where(leads, near, far))
        trail = parts(jnp.where(leads, far, near))
        change = product(lead, lead_parts, NN) + product(trail, trail_parts, NN)
        out_ref[pl.ds(row, 256), :] = tiles_ref[pl.ds(row, 256), :] - change


def products(where, chunks, tiles):
    cross = pl.pallas_call(
        cross_kernel,
        out_shape=jax.ShapeDtypeStruct((256, 256), jnp.float32),
        in_specs=[SMEM] + [VMEM] * 9,
        out_specs=VMEM,
        cost_estimate=pl.CostEstimate(flops=14_000_000_000, bytes_accessed=2300000, transcendentals=0),
        compiler_params=pltpu.CompilerParams(vmem_limit_bytes=LIMIT),
        name="cross",
    )(where, *chunks)
    half = jax.ShapeDtypeStruct((768, 128), jnp.float32)
    return pl.pallas_call(
        products_kernel,
        out_shape=(half, half),
        in_specs=[SMEM] + [VMEM] * 11,
        out_specs=(VMEM, VMEM),
        scratch_shapes=[pltpu.VMEM((2, 256, 256), jnp.float32)],
        cost_estimate=pl.CostEstimate(flops=800000000, bytes_accessed=4000000, transcendentals=0),
        compiler_params=pltpu.CompilerParams(vmem_limit_bytes=LIMIT),
        name="products",
    )(where, cross, *chunks, tiles)


def update(where, chunks, tiles, total, factors):
    return pl.pallas_call(
        update_kernel,
        out_shape=jax.ShapeDtypeStruct(tiles.shape, jnp.float32),
        in_specs=[SMEM] + [VMEM] * 12,
        out_specs=VMEM,
        cost_estimate=pl.CostEstimate(flops=1000000000, bytes_accessed=5000000, transcendentals=0),
        compiler_params=pltpu.CompilerParams(vmem_limit_bytes=LIMIT),
        name="update",
    )(where, *chunks, tiles, total, factors)


def shift(value, by):
    count = lax.axis_size("z")
    return lax.ppermute(value, "z", [(slot, (slot + by) % count) for slot in range(count)])


def owner_quarters(local):
    quarter = local.shape[0] // 4
    last = lax.axis_index("z") == lax.axis_size("z") - 1
    starts = [jnp.where(last, (3 - step) * quarter, step * quarter) for step in range(4)]
    return [lax.dynamic_slice_in_dim(local, start, quarter) for start in starts]


def scatter_quarters(pieces):
    slot = lax.axis_index("z")
    last = lax.axis_size("z") - 1
    chunk = pieces[0]
    for step in range(1, 4):
        piece = lax.ppermute(pieces[step], "z", [(0, step), (last, last - step)])
        chunk = jnp.where((slot == step) | (slot == last - step), piece, chunk)
    return chunk


def gather_panels(chunk):
    rows = chunk.shape[0]
    before2, after2 = shift(chunk, 2), shift(chunk, -2)
    before1, after1 = shift(chunk, 1), shift(chunk, -1)
    after3, before3 = shift(after2, -1), shift(before2, 1)
    upper, lower = shift(after2[: rows // 2], -2), shift(before2[rows // 2 :], 2)
    return [chunk, after1, after2, after3, upper, before3, before2, before1, lower]


def reduce_rows(other, mine):
    part = mine + lax.ppermute(other, "c", [(0, 1), (1, 0)])
    rows, columns = part.shape
    planes = lax.axis_size("x") * lax.axis_size("y")
    pieces = part.reshape(planes, rows // planes, columns)
    pieces = lax.all_to_all(pieces, PLANE, split_axis=0, concat_axis=0, tiled=True)
    pieces = jnp.broadcast_to(pieces.sum(0)[None], pieces.shape)
    pieces = lax.all_to_all(pieces, PLANE, split_axis=0, concat_axis=0, tiled=True)
    return lax.all_gather(pieces.reshape(rows, columns), "c", axis=1, tiled=True)


def per_device(eigvecs, panels, tfactors, owners):
    chunk = scatter_quarters(owner_quarters(panels[0]))
    where = jnp.stack([lax.axis_index("z"), jnp.where(owners[0] == 0, 0, 1), lax.axis_index("c")]).astype(jnp.int32)
    count = lax.axis_size("z")
    tiles = eigvecs.reshape(eigvecs.shape[0], count, -1).swapaxes(0, 1)
    chunk, tiles, where = lax.optimization_barrier((chunk, tiles, where))
    tiles = lax.all_to_all(tiles, "z", split_axis=0, concat_axis=0, tiled=True)
    tiles = tiles.reshape(-1, tiles.shape[2])
    chunks = gather_panels(chunk)
    total = reduce_rows(*products(where, chunks, tiles))
    return update(where, chunks, tiles, total, tfactors)


def solution(mesh):
    split = Mesh(mesh.devices.reshape(4, 8, 2, 8), ("x", "y", "c", "z"))
    rows = ("x", "y", "c")
    placed = (P(rows + ("z",), None), P("z", rows, None), P(), P())
    return jax.shard_map(per_device, mesh=split, in_specs=placed, out_specs=P(rows, "z"), check_vma=False)
```
